512 devices in a mesh: row: 16 (over x, y), col: 32 (over z, core).
Axes of the slice: x: 4, y: 4, z: 16, core: 2. Of those that a mesh axis runs over, the one named last changes fastest.
Arguments:
- member_outputs: float32 [3, 8192, 512], P(None, ('row', 'col')), may hold values from -6 to 6
- pivot_inverse_matrices: bfloat16 [2, 8192, 8192], P(None, 'col', 'row'), may hold values from -1 to 1.25, as said below
- former_subdiagonal_tiles: bfloat16 [2, 8192, 8192], P(None, 'row', 'col'), may hold values from -0.125 to 0.125
- latter_subdiagonal_tiles: bfloat16 [1, 8192, 8192], P(None, 'row', 'col'), may hold values from -0.125 to 0.125
Outputs:
- whitened: bfloat16 [2, 8192, 512], P(None, 'col')
- trailing: float32 [1, 8192, 512], P(None, ('row', 'col'))
- projections: float32 [256, 512], replicated
The draws below stay inside these ranges and needn't reach their ends.
Inputs may be any that keep to these rules, and one draw needn't show every extreme that they name: `pivot_inverse_matrices`: each block is lower triangular with a positive diagonal: the inverse of a diagonal block of the error covariance's Cholesky factor.
All inputs are finite; a program needn't handle non-finite values.
Results may differ from the reference program's by a relative error of at most 0.0057.
Values may be sent and summed in bfloat16 or wider, within the bound.
No kernel may reach another device: no remote copies, remote signals or barrier semaphores. Data moves between devices by JAX's collectives and lax.ppermute only.
A program may use at most 64 MiB of HBM per device.

```python
import jax
import jax.numpy as jnp
from jax import lax

MEASURES_PER_TILE = 8192
MEMBER_NUMBER = 256
SPAN_TILE_NUMBER = 3


def draw_pivot_inverse_matrices(key, part):
    key_off = jax.random.fold_in(key, 11)
    key_diag = jax.random.fold_in(key, 12)
    entries = jnp.clip(jax.random.normal(key_off, (2, MEASURES_PER_TILE, MEASURES_PER_TILE), jnp.float32), -6.0, 6.0)
    diagonal = 0.8 + 0.4 * jax.random.uniform(key_diag, (2, MEASURES_PER_TILE, 1), jnp.float32)
    row_index = lax.broadcasted_iota(jnp.int32, (MEASURES_PER_TILE, MEASURES_PER_TILE), 0)
    col_index = lax.broadcasted_iota(jnp.int32, (MEASURES_PER_TILE, MEASURES_PER_TILE), 1)
    lower = (col_index < row_index).astype(jnp.float32)
    identity = (col_index == row_index).astype(jnp.float32)
    values = entries * lower * (0.7 / jnp.sqrt(jnp.float32(MEASURES_PER_TILE))) + identity * diagonal
    return values.astype(jnp.bfloat16)


def with_spikes(array, rng, source, target, shards_of, factor):
    def block_of(position):
        return (jnp.arange(array.shape[position]) // (array.shape[position] // shards_of)).reshape((-1,) + (1,) * (array.ndim - 1 - position))

    near = jax.random.permutation(rng, shards_of)[block_of(target)]
    far = (block_of(target) + shards_of // 2) % shards_of
    return jnp.where((block_of(source) == near) | (block_of(source) == far), factor * array, array)


def levels(stream_key, dims, shards, low, high):
    gain, own = 1.0, jax.random.fold_in(stream_key, 6)
    for dim, shards_of in shards:
        heights = jnp.exp(jax.random.uniform(jax.random.fold_in(own, dim), (shards_of,), jnp.float32, low / len(shards), high / len(shards)))
        gain = gain * jnp.repeat(heights, dims[dim] // shards_of).reshape([-1 if axis == dim else 1 for axis in range(len(dims))])
    return gain


def normal_values(own_key, extent, scale, reach, pieces=(), dtype=jnp.bfloat16):
    array = scale * jax.random.normal(own_key, extent, jnp.float32)
    if pieces:
        array = array * levels(own_key, extent, pieces, -0.22, 0.18)
    return jnp.clip(array, -reach, reach).astype(dtype)


def bell_draw_with(stream_key, dims, width, limit, split, heavy, held_as=jnp.bfloat16):
    drawn = width * jax.random.normal(stream_key, dims, jnp.float32)
    if split:
        drawn = drawn * levels(stream_key, dims, split, -0.22, 0.18)
    return jnp.clip(with_spikes(drawn, jax.random.fold_in(stream_key, 3), *heavy), -limit, limit).astype(held_as)


def setup_inputs(seed: int = 0) -> dict:
    keys = jax.random.split(jax.random.key(seed), 5)
    member_outputs = normal_values(keys[0], (SPAN_TILE_NUMBER, MEASURES_PER_TILE, 2 * MEMBER_NUMBER), 1.0, 6.0, ((1, 512),), jnp.float32)
    pivot_inverse_matrices = draw_pivot_inverse_matrices(jax.random.fold_in(keys[4], 71), 0)
    former_subdiagonal_tiles = bell_draw_with(keys[2], (SPAN_TILE_NUMBER - 1, MEASURES_PER_TILE, MEASURES_PER_TILE), MEASURES_PER_TILE ** -0.5, 0.125, ((1, 16), (2, 32)), (2, 1, 32, 2.75))
    latter_subdiagonal_tiles = bell_draw_with(keys[3], (SPAN_TILE_NUMBER - 2, MEASURES_PER_TILE, MEASURES_PER_TILE), MEASURES_PER_TILE ** -0.5, 0.125, ((1, 16), (2, 32)), (2, 1, 32, 2.75))
    return {"member_outputs": member_outputs, "pivot_inverse_matrices": pivot_inverse_matrices, "former_subdiagonal_tiles": former_subdiagonal_tiles, "latter_subdiagonal_tiles": latter_subdiagonal_tiles}


def stripe_aggregate(panel_tiles, white_bf):
    def one_tile(tile):
        return jnp.dot(tile, white_bf, preferred_element_type=jnp.float32)
    return lax.map(one_tile, panel_tiles)


def reference(member_outputs, pivot_inverse_matrices, former_subdiagonal_tiles, latter_subdiagonal_tiles):
    initial_clipped_factor = member_outputs[0].astype(jnp.bfloat16)
    white_first = jnp.dot(pivot_inverse_matrices[0], initial_clipped_factor, preferred_element_type=jnp.float32)
    starting_cheap_cholesky = white_first.astype(jnp.bfloat16)
    fresh_strip_entries = member_outputs[1:] - stripe_aggregate(former_subdiagonal_tiles, starting_cheap_cholesky)
    second_rounded = fresh_strip_entries[0].astype(jnp.bfloat16)
    white_second = jnp.dot(pivot_inverse_matrices[1], second_rounded, preferred_element_type=jnp.float32)
    later_narrow_piece = white_second.astype(jnp.bfloat16)
    trailing = fresh_strip_entries[1:] - stripe_aggregate(latter_subdiagonal_tiles, later_narrow_piece)
    whitened = jnp.stack([starting_cheap_cholesky, later_narrow_piece])
    projections = jnp.dot(starting_cheap_cholesky[:, :MEMBER_NUMBER].T, starting_cheap_cholesky, preferred_element_type=jnp.float32)
    projections = projections + jnp.dot(later_narrow_piece[:, :MEMBER_NUMBER].T, later_narrow_piece, preferred_element_type=jnp.float32)
    return whitened, trailing, projections
```

```python
import jax
import jax.numpy as jnp
from jax import lax
from jax.sharding import Mesh, PartitionSpec as P

BF = jnp.bfloat16
F32 = jnp.float32
ROW = ("x", "y")


def swap(pieces, axis):
    return lax.all_to_all(pieces, axis, 0, 0)


def spread(piece, axis, count):
    return swap(jnp.broadcast_to(piece[None], (count,) + piece.shape), axis)


def fold(partial, axis, count):
    rows, width = partial.shape
    pieces = partial.astype(BF).reshape(count, rows // count, width)
    return jnp.sum(swap(pieces, axis).astype(F32), axis=0)


def both_cores(block):
    return lax.all_gather(block, "core", axis=0)


def body(outputs, inverses, former, latter):
    core = lax.axis_index("core")
    here = lax.axis_index(ROW)
    half = outputs.shape[2] // 2
    own = outputs.shape[1]

    def mine(pair):
        width = pair.shape[-1] // 2
        return lax.dynamic_slice_in_dim(pair, core * width, width, axis=pair.ndim - 1)

    def whiten(inverse, rows):
        partial = jnp.dot(inverse, rows, preferred_element_type=F32)
        piece = fold(partial, ROW, 16).astype(BF)
        return spread(piece, ROW, 16).reshape(-1, half)

    def panel(tiles, white):
        depth = tiles.shape[2]
        return jnp.dot(tiles[0], white[:depth], preferred_element_type=F32) + jnp.dot(
            tiles[1], white[depth:], preferred_element_type=F32
        )

    pair = mine(both_cores(outputs[:2]))
    height = 2 * own
    first_rows = pair[:, 0].reshape(height, half)
    second_rows = pair[:, 1].reshape(height, half)
    inverse0 = both_cores(inverses[0]).reshape(-1, inverses.shape[2])
    inverse1 = both_cores(inverses[1]).reshape(-1, inverses.shape[2])
    former0 = both_cores(former[0])
    former1 = both_cores(former[1])
    latter0 = both_cores(latter[0])

    gathered = spread(first_rows.astype(BF), "z", 16).reshape(-1, half)
    white0 = whiten(inverse0, gathered)
    update = fold(panel(former0, white0), "z", 16)
    right = (second_rows - update).astype(BF)
    gathered = spread(right, "z", 16).reshape(-1, half)
    white1 = whiten(inverse1, gathered)
    last = panel(former1, white0) + panel(latter0, white1)

    whole0 = both_cores(white0)
    whole1 = both_cores(white1)
    gram = lax.dot_general(whole0[0], white0, (((0,), (0,)), ((), ())), preferred_element_type=F32)
    gram = gram + lax.dot_general(
        whole1[0], white1, (((0,), (0,)), ((), ())), preferred_element_type=F32
    )
    part = half // 16
    slab = lax.dynamic_slice_in_dim(gram, here * part, part, axis=0).astype(BF)

    pieces = jnp.concatenate(
        [
            last.astype(BF).reshape(16, height, half),
            jnp.broadcast_to(slab[None], (16, part, half)),
        ],
        axis=1,
    )
    summed = jnp.sum(swap(pieces, "z").astype(F32), axis=0)
    ends = swap(summed[:height].reshape(2, own, half), "core")
    trailing = outputs[2:] - jnp.concatenate([ends[0], ends[1]], axis=1)[None]
    slabs = spread(summed[height:], ROW, 16).reshape(-1, half)
    halves = both_cores(slabs)
    projections = jnp.concatenate([halves[0], halves[1]], axis=1)

    rows = white0.shape[0] // 2
    stacked = jnp.stack([whole0, whole1])
    blocks = lax.dynamic_slice_in_dim(stacked, core * rows, rows, axis=2)
    whitened = jnp.concatenate([blocks[:, 0], blocks[:, 1]], axis=2)
    return (whitened, trailing, projections)


def solution(mesh):
    grid = Mesh(mesh.devices.reshape(4, 4, 16, 2), ("x", "y", "z", "core"))
    col = ("z", "core")
    every = ("x", "y", "z", "core")
    in_specs = (P(None, every, None), P(None, col, ROW), P(None, ROW, col), P(None, ROW, col))
    out_specs = (P(None, col, None), P(None, every, None), P())
    return jax.shard_map(body, mesh=grid, in_specs=in_specs, out_specs=out_specs, check_vma=False)
```

```python
import jax
import jax.numpy as jnp
from jax import lax
from jax.sharding import Mesh, PartitionSpec as P

BF = jnp.bfloat16
F32 = jnp.float32
ROW = ("x", "y")
COL = ("z", "core")
together = lax.optimization_barrier


def swap(pieces, axis):
    return lax.all_to_all(pieces, axis, 0, 0)


def spread(piece, axis, count):
    return swap(jnp.broadcast_to(piece[None], (count,) + piece.shape), axis)


def cut(partial, count):
    rows, width = partial.shape
    return partial.astype(BF).reshape(count, rows // count, width)


def total(pieces):
    return together(jnp.sum(pieces.astype(F32), axis=0))


def both_cores(block):
    return lax.all_gather(block, "core", axis=0)


def body(outputs, inverses, former, latter):
    core = lax.axis_index("core")
    here = lax.axis_index(ROW)
    half = outputs.shape[2] // 2
    own = outputs.shape[1]
    height = 2 * own

    def whiten(inverse, rows):
        partial = jnp.dot(inverse, rows, preferred_element_type=F32)
        piece = total(swap(cut(partial, 16), ROW)).astype(BF)
        return spread(piece, ROW, 16).reshape(-1, half)

    def panel(tiles, white):
        depth = tiles.shape[2]
        return jnp.dot(tiles[0], white[:depth], preferred_element_type=F32) + jnp.dot(
            tiles[1], white[depth:], preferred_element_type=F32
        )

    def gram(whole, white):
        return lax.dot_general(
            whole[0], white, (((0,), (0,)), ((), ())), preferred_element_type=F32
        )

    def block(whole):
        rows = whole.shape[1] // 2
        mine = lax.dynamic_slice_in_dim(whole, core * rows, rows, axis=1)
        return jnp.concatenate([mine[0], mine[1]], axis=1)

    first = outputs[0].astype(BF)
    first = jnp.stack([first[:, :half], first[:, half:]])
    pieces = jnp.broadcast_to(first[None], (16,) + first.shape).reshape(32, own, half)
    gathered = swap(pieces, COL).reshape(-1, half)
    (gathered, inverse0, inverse1, former0, former1, latter0, pair) = together(
        (
            gathered,
            both_cores(inverses[0]),
            both_cores(inverses[1]),
            both_cores(former[0]),
            both_cores(former[1]),
            both_cores(latter[0]),
            both_cores(outputs[1]),
        )
    )
    second = lax.dynamic_slice_in_dim(pair, core * half, half, axis=2).reshape(height, half)

    white0 = whiten(inverse0.reshape(-1, inverse0.shape[2]), gathered)
    pieces = swap(cut(panel(former0, white0), 16), "z")
    whole0 = both_cores(white0)
    pieces, last, slabs0, block0 = together(
        (pieces, panel(former1, white0), gram(whole0, white0), block(whole0))
    )
    right = (second - total(pieces)).astype(BF)
    gathered = spread(right, "z", 16).reshape(-1, half)
    white1 = whiten(inverse1.reshape(-1, inverse1.shape[2]), gathered)

    whole1 = both_cores(white1)
    last = last + panel(latter0, white1)
    slabs = slabs0 + gram(whole1, white1)
    part = half // 16
    slab = lax.dynamic_slice_in_dim(slabs, here * part, part, axis=0).astype(BF)
    pieces = jnp.concatenate(
        [cut(last, 16), jnp.broadcast_to(slab[None], (16, part, half))], axis=1
    )
    pieces, whole1 = together((swap(pieces, "z"), whole1))
    slab = total(pieces[:, height:])
    ends = total(pieces[:, :height])
    ends = lax.dynamic_slice_in_dim(both_cores(ends), core * own, own, axis=1)
    trailing = outputs[2:] - jnp.concatenate([ends[0], ends[1]], axis=1)[None]
    parts, trailing = together((spread(slab, ROW + ("core",), 32), trailing))
    parts = parts.reshape(16, 2, part, half)
    projections = jnp.concatenate(
        [parts[:, 0].reshape(half, half), parts[:, 1].reshape(half, half)], axis=1
    )
    whitened = jnp.stack([block0, block(whole1)])
    return (whitened, trailing, projections)


def solution(mesh):
    grid = Mesh(mesh.devices.reshape(4, 4, 16, 2), ("x", "y", "z", "core"))
    every = ("x", "y", "z", "core")
    in_specs = (P(None, every, None), P(None, COL, ROW), P(None, ROW, COL), P(None, ROW, COL))
    out_specs = (P(None, COL, None), P(None, every, None), P())
    return jax.shard_map(body, mesh=grid, in_specs=in_specs, out_specs=out_specs, check_vma=False)
```

```python
import jax
import jax.numpy as jnp
from jax import lax
from jax.sharding import Mesh, PartitionSpec as P

BF = jnp.bfloat16
F32 = jnp.float32
ROW = ("x", "y")
QUAD = ("pair", "core")
together = lax.optimization_barrier


def dot(a, b):
    return jnp.dot(a, b, preferred_element_type=F32)


def swap(pieces, axis):
    return lax.all_to_all(pieces, axis, 0, 0)


def spread(piece, axis, count):
    return swap(jnp.broadcast_to(piece[None], (count,) + piece.shape), axis)


def cut(partial, count):
    rows, width = partial.shape
    return partial.astype(BF).reshape(count, rows // count, width)


def total(pieces):
    return together(jnp.sum(pieces.astype(F32), axis=0))


def both_cores(block):
    return lax.all_gather(block, "core", axis=0)


def trade(block):
    return lax.ppermute(block, "pair", [(0, 1), (1, 0)])


def body(outputs, inverses, former, latter):
    core = lax.axis_index("core")
    side = lax.axis_index("pair")
    here = lax.axis_index(ROW)
    own = outputs.shape[1]
    half = outputs.shape[2] // 2
    quarter = half // 2
    tall = 2 * inverses.shape[1]

    def near(rows):
        depth = rows.shape[0] // 2
        return lax.dynamic_slice_in_dim(rows, side * depth, depth, axis=0)

    def far(rows):
        depth = rows.shape[0] // 2
        return lax.dynamic_slice_in_dim(rows, (1 - side) * depth, depth, axis=0)

    def beside(kept, got):
        return jnp.where(
            side == 0,
            jnp.concatenate([kept, got], axis=1),
            jnp.concatenate([got, kept], axis=1),
        )

    def panel(tiles, rows):
        depth = tiles.shape[2]
        return dot(tiles[0], rows[:depth]) + dot(tiles[1], rows[depth:])

    def panels(kept, got, white):
        return panel(kept, near(white)) + panel(got, far(white))

    def upright(pieces):
        return pieces.reshape(16, 2, -1, quarter).swapaxes(0, 1).reshape(2 * tall, quarter)

    def columns(whole):
        rows = whole.shape[1] // 2
        mine = lax.dynamic_slice_in_dim(whole, core * rows, rows, axis=1)
        return jnp.concatenate([mine[0], mine[1]], axis=1)

    first = both_cores(outputs[0].astype(BF))
    first = lax.dynamic_slice_in_dim(first, core * half, half, axis=2).reshape(2 * own, half)
    gathered = spread(first, ("eight", "pair"), 16).reshape(-1, half)
    given = trade(outputs[1])
    given = jnp.where(side == 0, jnp.stack([outputs[1], given]), jnp.stack([given, outputs[1]]))
    given = lax.dynamic_slice_in_dim(
        both_cores(given), core * half + side * quarter, quarter, axis=3
    )
    second = given.swapaxes(0, 1).reshape(4 * own, quarter)
    gathered, inverse0, second, former0, inverse1 = together(
        (gathered, both_cores(inverses[0]), second, former[0], inverses[1])
    )

    partial = dot(inverse0.reshape(tall, -1), gathered)
    pieces = swap(cut(partial, 16), ROW)
    pieces, former0_near, former0_got, inverse1_got, former1, latter0 = together(
        (pieces, both_cores(former0), trade(former0), trade(inverse1), former[1], latter[0])
    )
    piece = total(pieces).astype(BF)
    piece = jnp.stack([piece[:, :quarter], piece[:, quarter:]])
    pieces = jnp.broadcast_to(piece[None], (16,) + piece.shape)
    pieces = swap(pieces.reshape((32,) + piece.shape[1:]), ROW + ("pair",))
    pieces, former0_far, inverse1_near, former1_got, latter0_got = together(
        (
            pieces,
            both_cores(former0_got),
            both_cores(inverse1),
            trade(former1),
            trade(latter0),
        )
    )
    white0 = upright(pieces)

    pieces = swap(cut(panels(former0_near, former0_far, white0), 8), "eight")
    last = panels(both_cores(former1), both_cores(former1_got), white0)
    pieces, last, inverse1_far = together((pieces, last, both_cores(inverse1_got)))
    right = (second - total(pieces)).astype(BF)
    gathered = spread(right, "eight", 8).reshape(-1, quarter)
    gathered, latter0_near, latter0_far = together(
        (gathered, both_cores(latter0), both_cores(latter0_got))
    )

    pieces = jnp.concatenate(
        [
            cut(dot(inverse1_near.reshape(tall, -1), gathered), 16),
            cut(dot(inverse1_far.reshape(tall, -1), gathered), 16),
        ],
        axis=1,
    )
    pieces, got0 = together((swap(pieces, ROW), trade(far(white0))))
    piece = total(pieces).astype(BF).reshape(2, -1, quarter)
    piece = jnp.where(side == 0, piece, piece[::-1]).reshape(-1, quarter)
    pieces, block0 = together(
        (spread(piece, ROW, 16), columns(both_cores(beside(near(white0), got0))))
    )
    white1 = upright(pieces)

    part = half // 16
    member = (here % 8) * part + lax.broadcasted_iota(jnp.int32, (part, quarter), 0)
    picked = lax.broadcasted_iota(jnp.int32, (part, quarter), 1) == member
    pick = jnp.where(picked & (side == here // 8), 1.0, 0.0).astype(BF)
    slices = jnp.concatenate(
        [
            lax.dot_general(pick, white, (((1,), (1,)), ((), ())), preferred_element_type=F32)
            for white in (white0, white1)
        ],
        axis=1,
    ).astype(BF)
    slices = spread(slices, QUAD, 4)
    last = last + panels(latter0_near, latter0_far, white1)
    slices = slices[0] + slices[2]
    slab = dot(slices[:, : 2 * tall], white0) + dot(slices[:, 2 * tall :], white1)

    pieces = jnp.concatenate(
        [cut(last, 8), jnp.broadcast_to(slab.astype(BF)[None], (8, part, quarter))], axis=1
    )
    got1 = trade(far(white1))
    pieces, block1 = together(
        (swap(pieces, "eight"), columns(both_cores(beside(near(white1), got1))))
    )
    height = 4 * own
    slab = total(pieces[:, height:]).astype(BF)
    ends = total(pieces[:, :height])
    ends = both_cores(beside(near(ends), trade(far(ends))))
    trailing = outputs[2:] - columns(ends)[None]
    parts, trailing = together((spread(slab, ROW + QUAD, 64), trailing))
    parts = parts.astype(F32).reshape(16, 4, part, quarter)
    projections = jnp.concatenate(
        [parts[:, place].reshape(half, quarter) for place in (0, 2, 1, 3)], axis=1
    )
    return (jnp.stack([block0, block1]), trailing, projections)


def solution(mesh):
    axes = ("x", "y", "eight", "pair", "core")
    grid = Mesh(mesh.devices.reshape(4, 4, 8, 2, 2), axes)
    col = axes[2:]
    in_specs = (P(None, axes, None), P(None, col, ROW), P(None, ROW, col), P(None, ROW, col))
    out_specs = (P(None, col, None), P(None, axes, None), P())
    return jax.shard_map(body, mesh=grid, in_specs=in_specs, out_specs=out_specs, check_vma=False)
```

```python
import jax
import jax.numpy as jnp
from jax import lax
from jax.sharding import Mesh, PartitionSpec as P

BF = jnp.bfloat16
F32 = jnp.float32
ROW = ("x", "y")
COL = ("z", "core")
together = lax.optimization_barrier


def swap(pieces, axis):
    return lax.all_to_all(pieces, axis, 0, 0)


def spread(piece, axis, count):
    return swap(jnp.broadcast_to(piece[None], (count,) + piece.shape), axis)


def cut(partial, count):
    rows, width = partial.shape
    return partial.astype(BF).reshape(count, rows // count, width)


def total(pieces):
    return together(jnp.sum(pieces.astype(F32), axis=0))


def both_cores(block):
    return lax.all_gather(block, "core", axis=0)


def body(outputs, inverses, former, latter):
    core = lax.axis_index("core").astype(jnp.uint32)
    place = lax.axis_index(ROW).astype(jnp.uint32) * 16
    half = outputs.shape[2] // 2
    own = outputs.shape[1]
    height = 2 * own

    def whiten(inverse, rows):
        partial = jnp.dot(inverse, rows, preferred_element_type=F32)
        piece = total(swap(cut(partial, 16), ROW)).astype(BF)
        return spread(piece, ROW, 16).reshape(-1, half)

    def panel(tiles, white):
        depth = tiles.shape[2]
        return jnp.dot(tiles[0], white[:depth], preferred_element_type=F32) + jnp.dot(
            tiles[1], white[depth:], preferred_element_type=F32
        )

    def gram(whole, white):
        return lax.dot_general(
            whole[0], white, (((0,), (0,)), ((), ())), preferred_element_type=F32
        )

    def window(array, start, size, axis):
        starts = [jnp.uint32(0)] * array.ndim
        starts[axis] = start
        sizes = array.shape[:axis] + (size,) + array.shape[axis + 1 :]
        return lax.dynamic_slice(array, starts, sizes)

    def block(whole, start):
        sizes = (1, whole.shape[1] // 2, half)
        zero, one = jnp.uint32(0), jnp.uint32(1)
        left = lax.dynamic_slice(whole, (zero, start, zero), sizes)
        right = lax.dynamic_slice(whole, (one, start, zero), sizes)
        return jnp.concatenate([left[0], right[0]], axis=1)

    first = both_cores(outputs[0].astype(BF))
    first = window(first, core * half, half, 2).reshape(height, half)
    gathered = spread(first, "z", 16).reshape(-1, half)
    second = window(both_cores(outputs[1]), core * half, half, 2)
    rows = inverses.shape[1]
    gathered, inverse0, former0, second, block_start, end_start, slab_start = together(
        (
            gathered,
            both_cores(inverses[0]),
            both_cores(former[0]),
            second.reshape(height, half),
            core * rows,
            core * own,
            place,
        )
    )
    white0 = whiten(inverse0.reshape(-1, inverse0.shape[2]), gathered)

    pieces = cut(panel(former0, white0), 16)
    pieces, white0, former1, inverse1, latter0 = together(
        (pieces, white0, former[1], inverses[1], latter[0])
    )
    pieces = swap(pieces, "z")
    whole0 = both_cores(white0)
    last = panel(both_cores(former1), white0)
    pieces, last, slabs0, block0, inverse1, latter0 = together(
        (
            pieces,
            last,
            gram(whole0, white0),
            block(whole0, block_start),
            both_cores(inverse1),
            both_cores(latter0),
        )
    )
    right = (second - total(pieces)).astype(BF)
    gathered = spread(right, "z", 16).reshape(-1, half)
    white1 = whiten(inverse1.reshape(-1, inverse1.shape[2]), gathered)

    whole1 = both_cores(white1)
    last = last + panel(latter0, white1)
    slabs = slabs0 + gram(whole1, white1)
    part = half // 16
    slab = window(slabs, slab_start, part, 0).astype(BF)
    pieces = jnp.concatenate(
        [cut(last, 16), jnp.broadcast_to(slab[None], (16, part, half))], axis=1
    )
    pieces, whole1 = together((swap(pieces, "z"), whole1))
    slab = total(pieces[:, height:]).astype(BF)
    ends = total(pieces[:, :height])
    pieces, ends = together((jnp.broadcast_to(slab[None], (32,) + slab.shape), ends))
    trailing = outputs[2:] - block(both_cores(ends), end_start)[None]
    parts, trailing = together((swap(pieces, ROW + ("core",)), trailing))
    parts = parts.astype(F32).reshape(16, 2, part, half)
    projections = jnp.concatenate(
        [parts[:, 0].reshape(half, half), parts[:, 1].reshape(half, half)], axis=1
    )
    whitened = jnp.stack([block0, block(whole1, block_start)])
    return (whitened, trailing, projections)


def solution(mesh):
    grid = Mesh(mesh.devices.reshape(4, 4, 16, 2), ("x", "y", "z", "core"))
    every = ("x", "y", "z", "core")
    in_specs = (P(None, every, None), P(None, COL, ROW), P(None, ROW, COL), P(None, ROW, COL))
    out_specs = (P(None, COL, None), P(None, every, None), P())
    return jax.shard_map(body, mesh=grid, in_specs=in_specs, out_specs=out_specs, check_vma=False)
```

```python
import jax
import jax.numpy as jnp
from jax import lax
from jax.sharding import Mesh, PartitionSpec as P

BF = jnp.bfloat16
F32 = jnp.float32
ROW = ("x", "y")
COL = ("z", "core")
together = lax.optimization_barrier


def swap(pieces, axis):
    return lax.all_to_all(pieces, axis, 0, 0)


def spread(piece, axis, count):
    return swap(jnp.broadcast_to(piece[None], (count,) + piece.shape), axis)


def cut(partial, count):
    rows, width = partial.shape
    return partial.astype(BF).reshape(count, rows // count, width)


def total(pieces):
    return together(jnp.sum(pieces.astype(F32), axis=0))


def both_cores(block):
    return lax.all_gather(block, "core", axis=0)


def body(outputs, inverses, former, latter):
    core = lax.axis_index("core").astype(jnp.uint32)
    place = lax.axis_index(ROW).astype(jnp.uint32) * 16
    half = outputs.shape[2] // 2
    own = outputs.shape[1]
    height = 2 * own

    def whiten(inverse, rows):
        partial = jnp.dot(inverse, rows, preferred_element_type=F32)
        piece = total(swap(cut(partial, 16), ROW)).astype(BF)
        return spread(piece, ROW, 16).reshape(-1, half)

    def panel(tiles, white):
        depth = tiles.shape[2]
        return jnp.dot(tiles[0], white[:depth], preferred_element_type=F32) + jnp.dot(
            tiles[1], white[depth:], preferred_element_type=F32
        )

    def gram(whole, white):
        return lax.dot_general(
            whole[0], white, (((0,), (0,)), ((), ())), preferred_element_type=F32
        )

    def window(array, start, size, axis):
        starts = [jnp.uint32(0)] * array.ndim
        starts[axis] = start
        sizes = array.shape[:axis] + (size,) + array.shape[axis + 1 :]
        return lax.dynamic_slice(array, starts, sizes)

    def block(whole, start):
        sizes = (1, whole.shape[1] // 2, half)
        zero, one = jnp.uint32(0), jnp.uint32(1)
        left = lax.dynamic_slice(whole, (zero, start, zero), sizes)
        right = lax.dynamic_slice(whole, (one, start, zero), sizes)
        return jnp.concatenate([left[0], right[0]], axis=1)

    first = both_cores(outputs[0].astype(BF))
    first = window(first, core * half, half, 2).reshape(height, half)
    gathered = spread(first, "z", 16).reshape(-1, half)
    second = window(both_cores(outputs[1]), core * half, half, 2)
    rows = inverses.shape[1]
    gathered, inverse0, former0, second, inverse1, former1, *starts = together(
        (
            gathered,
            both_cores(inverses[0]),
            both_cores(former[0]),
            second.reshape(height, half),
            both_cores(inverses[1]),
            both_cores(former[1]),
            core * rows,
            core * own,
            place,
        )
    )
    block_start, end_start, slab_start = starts
    white0 = whiten(inverse0.reshape(-1, inverse0.shape[2]), gathered)

    pieces = cut(panel(former0, white0), 16)
    pieces, white0 = together((pieces, white0))
    pieces = swap(pieces, "z")
    last, white0, latter0 = together((panel(former1, white0), white0, latter[0]))
    whole0 = both_cores(white0)
    pieces, last, slabs0, block0, latter0 = together(
        (
            pieces,
            last,
            gram(whole0, white0),
            block(whole0, block_start),
            both_cores(latter0),
        )
    )
    right = (second - total(pieces)).astype(BF)
    gathered = spread(right, "z", 16).reshape(-1, half)
    white1 = whiten(inverse1.reshape(-1, inverse1.shape[2]), gathered)

    whole1 = both_cores(white1)
    last = last + panel(latter0, white1)
    slabs = slabs0 + gram(whole1, white1)
    part = half // 16
    slab = window(slabs, slab_start, part, 0).astype(BF)
    pieces = jnp.concatenate(
        [cut(last, 16), jnp.broadcast_to(slab[None], (16, part, half))], axis=1
    )
    pieces, whole1 = together((swap(pieces, "z"), whole1))
    slab = total(pieces[:, height:]).astype(BF)
    ends = total(pieces[:, :height])
    pieces, ends, whole1 = together((jnp.broadcast_to(slab[None], (32,) + slab.shape), ends, whole1))
    block1, ends = together((block(whole1, block_start), ends))
    trailing = outputs[2:] - block(both_cores(ends), end_start)[None]
    parts, trailing = together((swap(pieces, ROW + ("core",)), trailing))
    parts = parts.astype(F32).reshape(16, 2, part, half)
    projections = jnp.concatenate(
        [parts[:, 0].reshape(half, half), parts[:, 1].reshape(half, half)], axis=1
    )
    whitened = jnp.stack([block0, block1])
    return (whitened, trailing, projections)


def solution(mesh):
    grid = Mesh(mesh.devices.reshape(4, 4, 16, 2), ("x", "y", "z", "core"))
    every = ("x", "y", "z", "core")
    in_specs = (P(None, every, None), P(None, COL, ROW), P(None, ROW, COL), P(None, ROW, COL))
    out_specs = (P(None, COL, None), P(None, every, None), P())
    return jax.shard_map(body, mesh=grid, in_specs=in_specs, out_specs=out_specs, check_vma=False)
```

```python
import jax
import jax.numpy as jnp
from jax import lax
from jax.sharding import Mesh, PartitionSpec as P

BF = jnp.bfloat16
F32 = jnp.float32
ROW = ("x", "y")
COL = ("z", "core")
together = lax.optimization_barrier


def swap(pieces, axis):
    return lax.all_to_all(pieces, axis, 0, 0)


def spread(piece, axis, count):
    return swap(jnp.broadcast_to(piece[None], (count,) + piece.shape), axis)


def cut(partial, count):
    rows, width = partial.shape
    return partial.astype(BF).reshape(count, rows // count, width)


def total(pieces):
    return together(jnp.sum(pieces.astype(F32), axis=0))


def both_cores(block):
    return lax.all_gather(block, "core", axis=0)


def body(outputs, inverses, former, latter):
    core = lax.axis_index("core").astype(jnp.uint32)
    place = lax.axis_index(ROW).astype(jnp.uint32) * 16
    half = outputs.shape[2] // 2
    own = outputs.shape[1]
    height = 2 * own

    def whiten(inverse, rows):
        partial = jnp.dot(inverse, rows, preferred_element_type=F32)
        piece = total(swap(cut(partial, 16), ROW)).astype(BF)
        return spread(piece, ROW, 16).reshape(-1, half)

    def panel(tiles, white):
        depth = tiles.shape[2]
        return jnp.dot(tiles[0], white[:depth], preferred_element_type=F32) + jnp.dot(
            tiles[1], white[depth:], preferred_element_type=F32
        )

    def gram(whole, white):
        return lax.dot_general(
            whole[0], white, (((0,), (0,)), ((), ())), preferred_element_type=F32
        )

    def window(array, start, size, axis):
        starts = [jnp.uint32(0)] * array.ndim
        starts[axis] = start
        sizes = array.shape[:axis] + (size,) + array.shape[axis + 1 :]
        return lax.dynamic_slice(array, starts, sizes)

    def block(whole, start):
        sizes = (1, whole.shape[1] // 2, half)
        zero, one = jnp.uint32(0), jnp.uint32(1)
        left = lax.dynamic_slice(whole, (zero, start, zero), sizes)
        right = lax.dynamic_slice(whole, (one, start, zero), sizes)
        return jnp.concatenate([left[0], right[0]], axis=1)

    given = window(both_cores(outputs), core * half, half, 3)
    first = given[:, 0].astype(BF).reshape(height, half)
    gathered = spread(first, "z", 16).reshape(-1, half)
    second = given[:, 1]
    rows = inverses.shape[1]
    gathered, inverse0, former0, second, inverse1, former1, *starts = together(
        (
            gathered,
            both_cores(inverses[0]),
            both_cores(former[0]),
            second.reshape(height, half),
            both_cores(inverses[1]),
            both_cores(former[1]),
            core * rows,
            core * own,
            place,
        )
    )
    block_start, end_start, slab_start = starts
    white0 = whiten(inverse0.reshape(-1, inverse0.shape[2]), gathered)

    pieces = cut(panel(former0, white0), 16)
    pieces, white0 = together((pieces, white0))
    pieces = swap(pieces, "z")
    last, white0, latter0 = together((panel(former1, white0), white0, latter[0]))
    whole0 = both_cores(white0)
    pieces, last, slabs0, block0, latter0 = together(
        (
            pieces,
            last,
            gram(whole0, white0),
            block(whole0, block_start),
            both_cores(latter0),
        )
    )
    right = (second - total(pieces)).astype(BF)
    gathered = spread(right, "z", 16).reshape(-1, half)
    white1 = whiten(inverse1.reshape(-1, inverse1.shape[2]), gathered)

    whole1 = both_cores(white1)
    last = last + panel(latter0, white1)
    slabs = slabs0 + gram(whole1, white1)
    part = half // 16
    slab = window(slabs, slab_start, part, 0).astype(BF)
    pieces = jnp.concatenate(
        [cut(last, 16), jnp.broadcast_to(slab[None], (16, part, half))], axis=1
    )
    pieces, whole1 = together((swap(pieces, "z"), whole1))
    slab = total(pieces[:, height:]).astype(BF)
    ends = total(pieces[:, :height])
    pieces, ends, whole1 = together((jnp.broadcast_to(slab[None], (32,) + slab.shape), ends, whole1))
    block1, ends = together((block(whole1, block_start), ends))
    trailing = outputs[2:] - block(both_cores(ends), end_start)[None]
    parts, trailing = together((swap(pieces, ROW + ("core",)), trailing))
    parts = parts.astype(F32).reshape(16, 2, part, half)
    projections = jnp.concatenate(
        [parts[:, 0].reshape(half, half), parts[:, 1].reshape(half, half)], axis=1
    )
    whitened = jnp.stack([block0, block1])
    return (whitened, trailing, projections)


def solution(mesh):
    grid = Mesh(mesh.devices.reshape(4, 4, 16, 2), ("x", "y", "z", "core"))
    every = ("x", "y", "z", "core")
    in_specs = (P(None, every, None), P(None, COL, ROW), P(None, ROW, COL), P(None, ROW, COL))
    out_specs = (P(None, COL, None), P(None, every, None), P())
    return jax.shard_map(body, mesh=grid, in_specs=in_specs, out_specs=out_specs, check_vma=False)
```

```python
import jax
import jax.numpy as jnp
from jax import lax
from jax.sharding import Mesh, PartitionSpec as P

BF = jnp.bfloat16
F32 = jnp.float32
ROW = ("x", "y")
Z = ("eight", "pair")
COL = Z + ("core",)
together = lax.optimization_barrier


def swap(pieces, axis):
    return lax.all_to_all(pieces, axis, 0, 0)


def spread(piece, axis, count):
    return swap(jnp.broadcast_to(piece[None], (count,) + piece.shape), axis)


def cut(partial, count):
    rows, width = partial.shape
    return partial.astype(BF).reshape(count, rows // count, width)


def total(pieces):
    return together(jnp.sum(pieces.astype(F32), axis=0))


def both_cores(block):
    return lax.all_gather(block, "core", axis=0)


def body(outputs, inverses, former, latter):
    core = lax.axis_index("core").astype(jnp.uint32)
    place = lax.axis_index(ROW).astype(jnp.uint32) * 16
    half = outputs.shape[2] // 2
    own = outputs.shape[1]
    height = 2 * own

    def whiten(inverse, rows):
        partial = jnp.dot(inverse, rows, preferred_element_type=F32)
        piece = total(swap(cut(partial, 16), ROW)).astype(BF)
        return spread(piece, ROW, 16).reshape(-1, half)

    def panel(tiles, white):
        depth = tiles.shape[2]
        return jnp.dot(tiles[0], white[:depth], preferred_element_type=F32) + jnp.dot(
            tiles[1], white[depth:], preferred_element_type=F32
        )

    def gram(whole, white):
        return lax.dot_general(
            whole[0], white, (((0,), (0,)), ((), ())), preferred_element_type=F32
        )

    def window(array, start, size, axis):
        starts = [jnp.uint32(0)] * array.ndim
        starts[axis] = start
        sizes = array.shape[:axis] + (size,) + array.shape[axis + 1 :]
        return lax.dynamic_slice(array, starts, sizes)

    def block(whole, start):
        sizes = (1, whole.shape[1] // 2, half)
        zero, one = jnp.uint32(0), jnp.uint32(1)
        left = lax.dynamic_slice(whole, (zero, start, zero), sizes)
        right = lax.dynamic_slice(whole, (one, start, zero), sizes)
        return jnp.concatenate([left[0], right[0]], axis=1)

    given = window(both_cores(outputs), core * half, half, 3)
    first = given[:, 0].astype(BF).reshape(height, half)
    gathered = spread(first, Z, 16).reshape(-1, half)
    second = given[:, 1]
    rows = inverses.shape[1]
    gathered, inverse0, former0, second, inverse1, former1, *starts = together(
        (
            gathered,
            both_cores(inverses[0]),
            both_cores(former[0]),
            second.reshape(height, half),
            both_cores(inverses[1]),
            both_cores(former[1]),
            core * rows,
            core * own,
            place,
        )
    )
    block_start, end_start, slab_start = starts
    white0 = whiten(inverse0.reshape(-1, inverse0.shape[2]), gathered)

    pieces = cut(panel(former0, white0), 16)
    pieces, white0 = together((pieces, white0))
    pieces = swap(pieces, Z)
    last, white0, latter0 = together((panel(former1, white0), white0, latter[0]))
    whole0 = both_cores(white0)
    pieces, last, slabs0, block0, latter0 = together(
        (
            pieces,
            last,
            gram(whole0, white0),
            block(whole0, block_start),
            both_cores(latter0),
        )
    )
    right = (second - total(pieces)).astype(BF)
    gathered = spread(right, Z, 16).reshape(-1, half)
    white1 = whiten(inverse1.reshape(-1, inverse1.shape[2]), gathered)

    whole1 = both_cores(white1)
    last = last + panel(latter0, white1)
    slabs = slabs0 + gram(whole1, white1)
    part = half // 16
    slab = window(slabs, slab_start, part, 0).astype(BF)
    steps = last.astype(BF).reshape(8, 2, height, half).swapaxes(0, 1)
    pieces = jnp.concatenate(
        [
            steps.reshape(2, 8 * height, half),
            jnp.broadcast_to(slab[None], (2, part, half)),
        ],
        axis=1,
    )
    summed = total(swap(pieces, "pair")).astype(BF)
    pieces = jnp.concatenate(
        [
            summed[: 8 * height].reshape(8, height, half),
            jnp.broadcast_to(summed[None, 8 * height :], (8, part, half)),
        ],
        axis=1,
    )
    pieces, whole1 = together((swap(pieces, "eight"), whole1))
    slab = total(pieces[:, height:]).astype(BF)
    ends = total(pieces[:, :height])
    pieces, ends, whole1 = together((jnp.broadcast_to(slab[None], (32,) + slab.shape), ends, whole1))
    block1, ends = together((block(whole1, block_start), ends))
    trailing = outputs[2:] - block(both_cores(ends), end_start)[None]
    parts, trailing = together((swap(pieces, ROW + ("core",)), trailing))
    parts = parts.astype(F32).reshape(16, 2, part, half)
    projections = jnp.concatenate(
        [parts[:, 0].reshape(half, half), parts[:, 1].reshape(half, half)], axis=1
    )
    whitened = jnp.stack([block0, block1])
    return (whitened, trailing, projections)


def solution(mesh):
    every = ROW + COL
    grid = Mesh(mesh.devices.reshape(4, 4, 8, 2, 2), every)
    in_specs = (P(None, every, None), P(None, COL, ROW), P(None, ROW, COL), P(None, ROW, COL))
    out_specs = (P(None, COL, None), P(None, every, None), P())
    return jax.shard_map(body, mesh=grid, in_specs=in_specs, out_specs=out_specs, check_vma=False)
```

```python
import jax
import jax.numpy as jnp
from jax import lax
from jax.sharding import Mesh, PartitionSpec as P

BF = jnp.bfloat16
F32 = jnp.float32
ROW = "row"
COL = ("z", "core")
PLANE = ("row", "core")
FIRST = {"z": 8, ROW: 10, PLANE: 20}
together = lax.optimization_barrier


def swap(pieces, axis):
    count, first = pieces.shape[0], FIRST[axis]
    order = [(first + place) % count for place in range(count)]
    return lax.all_to_all(pieces, axis, 0, 0, axis_index_groups=[order])


def turn(pieces, by):
    return jnp.concatenate([pieces[by:], pieces[:by]], axis=0)


def spread(piece, axis, count):
    pieces = swap(jnp.broadcast_to(piece[None], (count,) + piece.shape), axis)
    return turn(pieces, count - FIRST[axis])


def cut(partial, axis):
    rows, width = partial.shape
    return turn(partial.astype(BF).reshape(16, rows // 16, width), FIRST[axis])


def total(pieces):
    return together(jnp.sum(pieces.astype(F32), axis=0))


def both_cores(block):
    return lax.all_gather(block, "core", axis=0)


def body(outputs, inverses, former, latter):
    core = lax.axis_index("core").astype(jnp.uint32)
    place = lax.axis_index(ROW).astype(jnp.uint32) * 16
    half = outputs.shape[2] // 2
    own = outputs.shape[1]
    height = 2 * own

    def whiten(inverse, rows):
        partial = jnp.dot(inverse, rows, preferred_element_type=F32)
        piece = total(swap(cut(partial, ROW), ROW)).astype(BF)
        return spread(piece, ROW, 16).reshape(-1, half)

    def panel(tiles, white):
        depth = tiles.shape[2]
        return jnp.dot(tiles[0], white[:depth], preferred_element_type=F32) + jnp.dot(
            tiles[1], white[depth:], preferred_element_type=F32
        )

    def gram(whole, white):
        return lax.dot_general(
            whole[0], white, (((0,), (0,)), ((), ())), preferred_element_type=F32
        )

    def window(array, start, size, axis):
        starts = [jnp.uint32(0)] * array.ndim
        starts[axis] = start
        sizes = array.shape[:axis] + (size,) + array.shape[axis + 1 :]
        return lax.dynamic_slice(array, starts, sizes)

    def block(whole, start):
        sizes = (1, whole.shape[1] // 2, half)
        zero, one = jnp.uint32(0), jnp.uint32(1)
        left = lax.dynamic_slice(whole, (zero, start, zero), sizes)
        right = lax.dynamic_slice(whole, (one, start, zero), sizes)
        return jnp.concatenate([left[0], right[0]], axis=1)

    given = window(both_cores(outputs), core * half, half, 3)
    first = given[:, 0].astype(BF).reshape(height, half)
    gathered = spread(first, "z", 16).reshape(-1, half)
    second = given[:, 1]
    rows = inverses.shape[1]
    gathered, inverse0, former0, second, inverse1, former1, *starts = together(
        (
            gathered,
            both_cores(inverses[0]),
            both_cores(former[0]),
            second.reshape(height, half),
            both_cores(inverses[1]),
            both_cores(former[1]),
            core * rows,
            core * own,
            place,
        )
    )
    block_start, end_start, slab_start = starts
    white0 = whiten(inverse0.reshape(-1, inverse0.shape[2]), gathered)

    pieces = cut(panel(former0, white0), "z")
    pieces, white0 = together((pieces, white0))
    pieces = swap(pieces, "z")
    last, white0, latter0 = together((panel(former1, white0), white0, latter[0]))
    whole0 = both_cores(white0)
    pieces, last, slabs0, block0, latter0 = together(
        (
            pieces,
            last,
            gram(whole0, white0),
            block(whole0, block_start),
            both_cores(latter0),
        )
    )
    right = (second - total(pieces)).astype(BF)
    gathered = spread(right, "z", 16).reshape(-1, half)
    white1 = whiten(inverse1.reshape(-1, inverse1.shape[2]), gathered)

    whole1 = both_cores(white1)
    last = last + panel(latter0, white1)
    slabs = slabs0 + gram(whole1, white1)
    part = half // 16
    slab = window(slabs, slab_start, part, 0).astype(BF)
    pieces = jnp.concatenate(
        [cut(last, "z"), jnp.broadcast_to(slab[None], (16, part, half))], axis=1
    )
    pieces, whole1 = together((swap(pieces, "z"), whole1))
    slab = total(pieces[:, height:]).astype(BF)
    ends = total(pieces[:, :height])
    pieces = jnp.broadcast_to(slab[None], (32,) + slab.shape)
    pieces, ends, whole1 = together((pieces, ends, whole1))
    block1, ends = together((block(whole1, block_start), ends))
    trailing = outputs[2:] - block(both_cores(ends), end_start)[None]
    parts, trailing = together((swap(pieces, PLANE), trailing))
    parts = turn(parts, 32 - FIRST[PLANE]).astype(F32).reshape(16, 2, part, half)
    projections = jnp.concatenate(
        [parts[:, 0].reshape(half, half), parts[:, 1].reshape(half, half)], axis=1
    )
    whitened = jnp.stack([block0, block1])
    return (whitened, trailing, projections)


def solution(mesh):
    grid = Mesh(mesh.devices.reshape(16, 16, 2), ("row", "z", "core"))
    every = ("row", "z", "core")
    in_specs = (P(None, every, None), P(None, COL, ROW), P(None, ROW, COL), P(None, ROW, COL))
    out_specs = (P(None, COL, None), P(None, every, None), P())
    return jax.shard_map(body, mesh=grid, in_specs=in_specs, out_specs=out_specs, check_vma=False)
```

```python
import jax
import jax.numpy as jnp
from jax import lax
from jax.sharding import Mesh, PartitionSpec as P

BF = jnp.bfloat16
F32 = jnp.float32
ROW = "row"
Z = ("eight", "pair")
COL = ("eight", "pair", "core")
PLANE = ("row", "core")
WIDE = ("row", "pair", "core")
FIRST = {Z: 8, ROW: 10, PLANE: 20, "eight": 4, "pair": 0, WIDE: 40}
together = lax.optimization_barrier


def swap(pieces, axis):
    count, first = pieces.shape[0], FIRST[axis]
    order = [(first + place) % count for place in range(count)]
    return lax.all_to_all(pieces, axis, 0, 0, axis_index_groups=[order])


def turn(pieces, by):
    return jnp.concatenate([pieces[by:], pieces[:by]], axis=0)


def spread(piece, axis, count):
    pieces = swap(jnp.broadcast_to(piece[None], (count,) + piece.shape), axis)
    return turn(pieces, count - FIRST[axis])


def cut(partial, axis):
    rows, width = partial.shape
    return turn(partial.astype(BF).reshape(16, rows // 16, width), FIRST[axis])


def total(pieces):
    return together(jnp.sum(pieces.astype(F32), axis=0))


def both_cores(block):
    return lax.all_gather(block, "core", axis=0)


def body(outputs, inverses, former, latter):
    core = lax.axis_index("core").astype(jnp.uint32)
    place = (lax.axis_index(ROW).astype(jnp.uint32) + 16 - FIRST[ROW]) % 16 * 16
    half = outputs.shape[2] // 2
    own = outputs.shape[1]
    height = 2 * own

    def whiten(inverse, rows):
        partial = jnp.dot(inverse, rows, preferred_element_type=F32)
        partial = partial.astype(BF).reshape(16, -1, half)
        piece = total(swap(partial, ROW)).astype(BF)
        pieces = jnp.broadcast_to(piece[None], (16,) + piece.shape)
        return swap(pieces, ROW).reshape(-1, half)

    def panel(tiles, white):
        depth = tiles.shape[2]
        return jnp.dot(tiles[0], white[:depth], preferred_element_type=F32) + jnp.dot(
            tiles[1], white[depth:], preferred_element_type=F32
        )

    def gram(whole, white):
        return lax.dot_general(
            whole[0], white, (((0,), (0,)), ((), ())), preferred_element_type=F32
        )

    def window(array, start, size, axis):
        starts = [jnp.uint32(0)] * array.ndim
        starts[axis] = start
        sizes = array.shape[:axis] + (size,) + array.shape[axis + 1 :]
        return lax.dynamic_slice(array, starts, sizes)

    def block(whole, start):
        sizes = (1, whole.shape[1] // 2, half)
        zero, one = jnp.uint32(0), jnp.uint32(1)
        left = lax.dynamic_slice(whole, (zero, start, zero), sizes)
        right = lax.dynamic_slice(whole, (one, start, zero), sizes)
        return jnp.concatenate([left[0], right[0]], axis=1)

    given = window(both_cores(outputs), core * half, half, 3)
    first = given[:, 0].astype(BF).reshape(height, half)
    gathered = spread(first, Z, 16).reshape(-1, half)
    second = given[:, 1]
    rows = inverses.shape[1]
    gathered, inverse0, former0, second, inverse1, former1, *starts = together(
        (
            gathered,
            both_cores(inverses[0]),
            both_cores(former[0]),
            second.reshape(height, half),
            both_cores(inverses[1]),
            both_cores(former[1]),
            core * rows,
            core * own,
            place,
        )
    )
    block_start, end_start, slab_start = starts
    white0 = whiten(inverse0.reshape(-1, inverse0.shape[2]), gathered)

    pieces = cut(panel(former0, white0), Z)
    pieces, white0 = together((pieces, white0))
    pieces = swap(pieces, Z)
    last, white0, latter0 = together((panel(former1, white0), white0, latter[0]))
    whole0 = both_cores(white0)
    pieces, last, slabs0, block0, latter0 = together(
        (
            pieces,
            last,
            gram(whole0, white0),
            block(whole0, block_start),
            both_cores(latter0),
        )
    )
    right = (second - total(pieces)).astype(BF)
    gathered = spread(right, Z, 16).reshape(-1, half)
    white1 = whiten(inverse1.reshape(-1, inverse1.shape[2]), gathered)

    whole1 = both_cores(white1)
    last = last + panel(latter0, white1)
    slabs = slabs0 + gram(whole1, white1)
    part = half // 16
    slab = window(slabs, slab_start, part, 0).astype(BF)
    steps = last.astype(BF).reshape(8, 2, height, half)
    steps = turn(steps, FIRST["eight"]).swapaxes(0, 1)
    pieces = jnp.concatenate(
        [
            steps.reshape(2, 8 * height, half),
            jnp.broadcast_to(slab[None], (2, part, half)),
        ],
        axis=1,
    )
    summed = total(swap(pieces, "pair")).astype(BF)
    pieces = jnp.concatenate(
        [
            summed[: 8 * height].reshape(8, height, half),
            jnp.broadcast_to(summed[None, 8 * height :], (8, part, half)),
        ],
        axis=1,
    )
    pieces, whole1 = together((swap(pieces, "eight"), whole1))
    slab = total(pieces[:, height:]).astype(BF)
    ends = total(pieces[:, :height])
    pieces = jnp.broadcast_to(slab[None], (32,) + slab.shape)
    pieces, ends, whole1 = together((pieces, ends, whole1))
    block1, ends = together((block(whole1, block_start), ends))
    trailing = outputs[2:] - block(both_cores(ends), end_start)[None]
    parts, trailing = together((swap(pieces, PLANE), trailing))
    parts = parts.astype(F32).reshape(16, 2, part, half)
    projections = jnp.concatenate(
        [parts[:, 0].reshape(half, half), parts[:, 1].reshape(half, half)], axis=1
    )
    whitened = jnp.stack([block0, block1])
    return (whitened, trailing, projections)


def solution(mesh):
    grid = Mesh(mesh.devices.reshape(16, 8, 2, 2), ("row", "eight", "pair", "core"))
    every = ("row",) + COL
    in_specs = (P(None, every, None), P(None, COL, ROW), P(None, ROW, COL), P(None, ROW, COL))
    out_specs = (P(None, COL, None), P(None, every, None), P())
    return jax.shard_map(body, mesh=grid, in_specs=in_specs, out_specs=out_specs, check_vma=False)
```

```python
import jax
import jax.numpy as jnp
from jax import lax
from jax.sharding import Mesh, PartitionSpec as P

BF = jnp.bfloat16
F32 = jnp.float32
ROW = "row"
Z = ("eight", "pair")
COL = ("eight", "pair", "core")
PLANE = ("row", "core")
WIDE = ("row", "pair", "core")
FIRST = {Z: 8, ROW: 10, PLANE: 20, "eight": 4, "pair": 0, WIDE: 40}
together = lax.optimization_barrier


def swap(pieces, axis):
    count, first = pieces.shape[0], FIRST[axis]
    order = [(first + place) % count for place in range(count)]
    return lax.all_to_all(pieces, axis, 0, 0, axis_index_groups=[order])


def turn(pieces, by):
    return jnp.concatenate([pieces[by:], pieces[:by]], axis=0)


def spread(piece, axis, count):
    return swap(jnp.broadcast_to(piece[None], (count,) + piece.shape), axis)


def cut(partial, axis):
    rows, width = partial.shape
    return turn(partial.astype(BF).reshape(16, rows // 16, width), FIRST[axis])


def total(pieces):
    return together(jnp.sum(pieces.astype(F32), axis=0))


def both_cores(block):
    return lax.all_gather(block, "core", axis=0)


def body(outputs, inverses, former, latter):
    core = lax.axis_index("core").astype(jnp.uint32)
    place = (lax.axis_index(ROW).astype(jnp.uint32) + 16 - FIRST[ROW]) % 16 * 16
    half = outputs.shape[2] // 2
    own = outputs.shape[1]
    height = 2 * own

    def whiten(inverse, rows):
        depth = rows.shape[0] // 2
        partial = jnp.dot(inverse[:, depth:], rows[:depth], preferred_element_type=F32)
        partial = partial + jnp.dot(inverse[:, :depth], rows[depth:], preferred_element_type=F32)
        partial = partial.astype(BF).reshape(16, -1, half)
        piece = total(swap(partial, ROW)).astype(BF)
        pieces = jnp.broadcast_to(piece[None], (16,) + piece.shape)
        return swap(pieces, ROW).reshape(-1, half)

    def panel(tiles, white):
        depth = tiles.shape[2]
        return jnp.dot(tiles[0], white[:depth], preferred_element_type=F32) + jnp.dot(
            tiles[1], white[depth:], preferred_element_type=F32
        )

    def gram(whole, white):
        return lax.dot_general(
            whole[0], white, (((0,), (0,)), ((), ())), preferred_element_type=F32
        )

    def window(array, start, size, axis):
        starts = [jnp.uint32(0)] * array.ndim
        starts[axis] = start
        sizes = array.shape[:axis] + (size,) + array.shape[axis + 1 :]
        return lax.dynamic_slice(array, starts, sizes)

    def block(whole, start):
        sizes = (1, whole.shape[1] // 2, half)
        zero, one = jnp.uint32(0), jnp.uint32(1)
        left = lax.dynamic_slice(whole, (zero, start, zero), sizes)
        right = lax.dynamic_slice(whole, (one, start, zero), sizes)
        return jnp.concatenate([left[0], right[0]], axis=1)

    given = window(both_cores(outputs), core * half, half, 3)
    first = given[:, 0].astype(BF).reshape(height, half)
    gathered = spread(first, Z, 16).reshape(-1, half)
    second = given[:, 1]
    rows = inverses.shape[1]
    gathered, inverse0, former0, second, inverse1, former1, *starts = together(
        (
            gathered,
            both_cores(inverses[0]),
            both_cores(former[0]),
            second.reshape(height, half),
            both_cores(inverses[1]),
            both_cores(former[1]),
            core * rows,
            core * own,
            place,
        )
    )
    block_start, end_start, slab_start = starts
    white0 = whiten(inverse0.reshape(-1, inverse0.shape[2]), gathered)

    pieces = cut(panel(former0, white0), Z)
    pieces, white0 = together((pieces, white0))
    pieces = swap(pieces, Z)
    last, white0, latter0 = together((panel(former1, white0), white0, latter[0]))
    whole0 = both_cores(white0)
    pieces, last, slabs0, block0, latter0 = together(
        (
            pieces,
            last,
            gram(whole0, white0),
            block(whole0, block_start),
            both_cores(latter0),
        )
    )
    right = (second - total(pieces)).astype(BF)
    gathered = spread(right, Z, 16).reshape(-1, half)
    white1 = whiten(inverse1.reshape(-1, inverse1.shape[2]), gathered)

    whole1 = both_cores(white1)
    last = last + panel(latter0, white1)
    slabs = slabs0 + gram(whole1, white1)
    part = half // 16
    slab = window(slabs, slab_start, part, 0).astype(BF)
    steps = last.astype(BF).reshape(8, 2, height, half)
    steps = turn(steps, FIRST["eight"]).swapaxes(0, 1)
    pieces = jnp.concatenate(
        [
            steps.reshape(2, 8 * height, half),
            jnp.broadcast_to(slab[None], (2, part, half)),
        ],
        axis=1,
    )
    summed = total(swap(pieces, "pair")).astype(BF)
    pieces = jnp.concatenate(
        [
            summed[: 8 * height].reshape(8, height, half),
            jnp.broadcast_to(summed[None, 8 * height :], (8, part, half)),
        ],
        axis=1,
    )
    pieces, whole1 = together((swap(pieces, "eight"), whole1))
    slab = total(pieces[:, height:]).astype(BF)
    ends = total(pieces[:, :height])
    pieces = jnp.broadcast_to(slab[None], (32,) + slab.shape)
    pieces, ends, whole1 = together((pieces, ends, whole1))
    block1, ends = together((block(whole1, block_start), ends))
    trailing = outputs[2:] - block(both_cores(ends), end_start)[None]
    parts, trailing = together((swap(pieces, PLANE), trailing))
    parts = parts.astype(F32).reshape(16, 2, part, half)
    projections = jnp.concatenate(
        [parts[:, 0].reshape(half, half), parts[:, 1].reshape(half, half)], axis=1
    )
    whitened = jnp.stack([block0, block1])
    return (whitened, trailing, projections)


def solution(mesh):
    grid = Mesh(mesh.devices.reshape(16, 8, 2, 2), ("row", "eight", "pair", "core"))
    every = ("row",) + COL
    in_specs = (P(None, every, None), P(None, COL, ROW), P(None, ROW, COL), P(None, ROW, COL))
    out_specs = (P(None, COL, None), P(None, every, None), P())
    return jax.shard_map(body, mesh=grid, in_specs=in_specs, out_specs=out_specs, check_vma=False)
```
